32 devices in a mesh: grp: 2 (over y), seq: 4 (over z), head: 4 (over x, core).
Axes of the slice: x: 2, y: 2, z: 4, core: 2. Of those that a mesh axis runs over, the one named last changes fastest.
Arguments:
- tokens: bfloat16 [1024, 2048], P(('grp', 'seq')), parts along dimension 0, may hold values from -6 to 6
- attn_weight: bfloat16 [4, 2048, 2048], P(None, 'seq', 'head'), may hold values from -0.125 to 0.125
- attn_gain: float32 [2048], replicated, may hold values from 0.25 to 1.75
- moe_gain: float32 [2048], replicated, may hold values from 0.25 to 1.75
- routes: int32 [1024, 8], P(('grp', 'seq')), parts along dimension 0, may hold values from 0 to 63, all different within a row; in each aligned block of 128 rows (0 to 127, 128 to 255, ...) at most 18 rows name the same one
- gates: float32 [1024, 8], P(('grp', 'seq')), parts along dimension 0, may hold values from 0.05 to 0.4
- expert_gate: bfloat16 [64, 2048, 1024], P('seq', None, 'head'), may hold values from -0.125 to 0.125
- expert_up: bfloat16 [64, 2048, 1024], P('seq', None, 'head'), may hold values from -0.125 to 0.125
- expert_down: bfloat16 [64, 1024, 2048], P('seq', 'head'), may hold values from -0.1875 to 0.1875
Outputs:
- mixed: bfloat16 [1024, 2048], P(('grp', 'seq')), parts along dimension 0
The draws below stay inside these ranges and needn't reach their ends.
There are 2 independent parts, one for each index of `grp`. The reference program is written for one: setup_inputs(seed, part) draws one part's arguments, and reference() takes and returns one part's arrays. A program takes and returns all parts, laid end to end along the dimension named above; an argument that names none is the same for every part. Nothing has to cross between parts.
Inputs may be any that keep to these rules, and one draw needn't show every extreme that they name: `routes`: in each aligned block of 128 tokens, no expert is named by more than 18 pairs of a token and a choice, a bound that some block reaches; a token's 8 experts differ.
All inputs are finite; a program needn't handle non-finite values.
Results may differ from the reference program's by a relative error of at most 0.015.
Values may be sent and summed in bfloat16 or wider, within the bound.
A program may use at most 128 MiB of HBM per device.

```python
import math
import jax
import jax.numpy as jnp
import numpy as np
from jax import lax

D = 2048
HEADS = 16
HEAD_DIM = 128
EXPERTS = 64
FFE = 1024
TOPK = 8
TOK_DEV = 128
CAP = 18
TOKENS = 512
N_SEQ = 4
N_HEAD = 4


def levels(key, shape, cuts, smallest, top_value):
    def one(dim, blocks):
        heights = jax.random.uniform(jax.random.fold_in(jax.random.fold_in(key, 6), dim), (blocks,), jnp.float32, smallest / len(cuts), top_value / len(cuts))
        return jnp.repeat(jnp.exp(heights), shape[dim] // blocks).reshape((-1,) + (1,) * (len(shape) - dim - 1))

    level = one(*cuts[0])
    for cut in cuts[1:]:
        level = level * one(*cut)
    return level


def shared_out(stream_key, own, number, rows, amount, top, most, skew):
    ranking = jax.random.permutation(stream_key, amount)
    heavy_load, ordinary = shares(amount, rows * top, most, skew, True), shares(amount, rows * top, most, skew, False)
    places = jnp.arange(amount)

    def named(sizes, offset_by):
        used = int((sizes > 0).sum())
        fixed = max(1, used // 4)
        shifted = fixed + (places - fixed + offset_by * (used - fixed)) % max(1, amount - fixed)
        return jnp.zeros((amount,), jnp.int32).at[ranking[jnp.where(places < fixed, places, shifted)]].set(jnp.asarray(sizes, jnp.int32))

    sizes = jnp.where(number % 4 == 0, named(heavy_load, number // 4), named(ordinary, number - number // 4 - 1))
    mixed = jax.random.permutation(jax.random.fold_in(own, 3), amount)
    source_of, receiver = mixed[0:amount // 2 * 2:2], mixed[1:amount // 2 * 2:2]
    slack = jnp.minimum(sizes[source_of] - 1, most - sizes[receiver]) // 2
    slack = jnp.where((source_of == ranking[0]) | (receiver == ranking[0]) | (sizes[receiver] == 0), 0, jnp.maximum(slack, 0))
    shifted = jax.random.randint(jax.random.fold_in(own, 4), (amount // 2,), 0, 1 << 20) % (slack + 1)
    sizes = sizes.at[source_of].add(-shifted).at[receiver].add(shifted)
    members = jnp.searchsorted(jnp.cumsum(sizes), jnp.arange(rows * top), side="right").astype(jnp.int32)
    table = members.reshape(top, rows).T
    table = table[jax.random.permutation(jax.random.fold_in(own, 1), rows)]
    offset_by = jax.random.randint(jax.random.fold_in(own, 2), (rows, 1), 0, top)
    return jnp.take_along_axis(table, (jnp.arange(top)[None, :] + offset_by) % top, axis=1)


def shares(count, total, limit, slope, full):
    portions = [(1 << 20) // math.isqrt(rank ** slope) + 1 for rank in range(1, count + 1)]
    largest = limit if full else min(limit, max(-(-total // count), total * portions[0] // sum(portions)))
    least = 1 if total - largest >= count - 1 else 0
    counts, spare = [largest] + [least] * (count - 1), total - largest - least * (count - 1)
    while spare > 0:
        movable = [i for i in range(1, count) if counts[i] < largest] or [i for i in range(1, count) if counts[i] < limit]
        whole, budget = sum([portions[i] for i in movable]), spare
        for i in movable:
            extra = min(limit - counts[i], max(1, budget * portions[i] // whole), spare)
            counts[i] = counts[i] + extra
            spare = spare - extra
    return np.array(counts)


def bell_draw(stream_key, shape, spread, bound, split=(), kind=jnp.bfloat16):
    drawn = jax.random.normal(stream_key, shape, jnp.float32) * spread
    if len(split) > 0:
        drawn = levels(stream_key, shape, split, -0.22, 0.18) * drawn
    return jnp.clip(drawn, min=-bound, max=bound).astype(kind)


def setup_inputs(seed: int = 0, part: int = 0) -> dict:
    keys = jax.random.split(jax.random.key(seed), 10)
    part_splits = jax.random.split(jax.random.fold_in(keys[9], part), 10)
    tokens = bell_draw(part_splits[0], (TOKENS, D), 1.0, 6.0, ((0, 4),))
    attn_weight = bell_draw(keys[1], (4, D, HEADS * HEAD_DIM), D ** -0.5, 0.125, ((1, 4), (2, 4)))
    attn_gain = jnp.clip(1.0 + 0.15 * jax.random.normal(keys[2], (D,), jnp.float32), 0.25, 1.75)
    moe_gain = jnp.clip(1.0 + 0.15 * jax.random.normal(keys[3], (D,), jnp.float32), 0.25, 1.75)
    routes_keys = jax.random.split(jax.random.fold_in(part_splits[4], 1), TOKENS // TOK_DEV)
    routes_turns = jax.random.permutation(jax.random.fold_in(part_splits[4], 3), TOKENS // TOK_DEV)
    routes = jax.vmap(lambda own, number: shared_out(jax.random.fold_in(part_splits[4], 2), own, number, TOK_DEV, EXPERTS, TOPK, CAP, 2))(routes_keys, routes_turns).reshape((TOKENS, TOPK))
    gates = jnp.clip(0.05 + 0.35 * jax.random.uniform(part_splits[5], (TOKENS, TOPK), jnp.float32) ** levels(part_splits[5], (TOKENS, TOPK), ((0, 4),), -0.2, 0.2), 0.05, 0.4)
    expert_gate = bell_draw(keys[6], (EXPERTS, D, FFE), D ** -0.5, 0.125, ((0, 4), (2, 4)))
    expert_up = bell_draw(keys[7], (EXPERTS, D, FFE), D ** -0.5, 0.125, ((0, 4), (2, 4)))
    expert_down = bell_draw(keys[8], (EXPERTS, FFE, D), FFE ** -0.5, 0.1875, ((0, 4), (1, 4)))
    return dict(tokens=tokens, attn_weight=attn_weight, attn_gain=attn_gain, moe_gain=moe_gain, routes=routes, gates=gates, expert_gate=expert_gate, expert_up=expert_up, expert_down=expert_down)


PRECISE = lax.Precision.HIGHEST

def rms_scale(row_block, gain_vec):
    widened = row_block.astype(jnp.float32)
    factor = lax.rsqrt(lax.optimization_barrier(jnp.mean(widened * widened, axis=-1, keepdims=True)) + 1e-06)
    return widened * factor * gain_vec

def head_norm(outputs):
    return outputs * lax.rsqrt(lax.optimization_barrier(jnp.mean(outputs * outputs, axis=-1, keepdims=True)) + 1e-06)

def causal_linear(query_rows, key_rows, value_rows):
    block_count = query_rows.shape[0] // TOK_DEV
    shaped = [matrix.reshape(block_count, TOK_DEV, HEADS, HEAD_DIM).astype(jnp.float32) for matrix in (query_rows, key_rows, value_rows)]
    lower_mask = jnp.arange(TOK_DEV)[:, None] >= jnp.arange(TOK_DEV)[None, :]

    def advance(carry_state, block):
        query_blk, key_blk, value_blk = block
        inter_part = jnp.einsum('thd,hde->the', query_blk, carry_state, precision=PRECISE)
        scores = jnp.einsum('thd,shd->hts', query_blk, key_blk, precision=PRECISE)
        scores = jnp.where(lower_mask[None], scores, 0.0)
        intra_part = jnp.einsum('hts,she->the', scores, value_blk, precision=PRECISE)
        carry_state = carry_state + jnp.einsum('thd,the->hde', key_blk, value_blk, precision=PRECISE)
        return (carry_state, inter_part + intra_part)
    start_state = jnp.zeros((HEADS, HEAD_DIM, HEAD_DIM), jnp.float32)
    final_state, outputs = lax.scan(advance, start_state, tuple(shaped))
    return outputs.reshape(block_count * TOK_DEV, HEADS, HEAD_DIM)

def slot_numbers(route_rows):
    one_hot = (route_rows[..., None] == jnp.arange(EXPERTS, dtype=jnp.int32)).astype(jnp.int32)
    earlier = jnp.cumsum(one_hot, axis=-2) - one_hot
    return route_rows * CAP + lax.optimization_barrier(jnp.sum(earlier * one_hot, axis=-1))

def expert_apply(slot_rows, gate_mat, up_mat, down_mat):
    gate_val = jnp.dot(slot_rows, gate_mat, preferred_element_type=jnp.float32)
    up_val = jnp.dot(slot_rows, up_mat, preferred_element_type=jnp.float32)
    hidden = (jax.nn.silu(gate_val) * up_val).astype(jnp.bfloat16)
    grouped = hidden.reshape(-1, N_HEAD, FFE // N_HEAD).astype(jnp.float32)
    down_groups = down_mat.reshape(N_HEAD, FFE // N_HEAD, D).astype(jnp.float32)
    partial_value = jnp.einsum('rgf,gfd->rgd', grouped, down_groups, precision=PRECISE).astype(jnp.bfloat16)
    return lax.optimization_barrier(jnp.sum(partial_value.astype(jnp.float32), axis=1))

def reference(tokens, attn_weight, attn_gain, moe_gain, routes, gates, expert_gate, expert_up, expert_down):
    total_rows = tokens.shape[0]
    normed = rms_scale(tokens, attn_gain).astype(jnp.bfloat16)
    projected = [jnp.dot(normed, attn_weight[which], preferred_element_type=jnp.float32).astype(jnp.bfloat16) for which in range(3)]
    outputs = causal_linear(projected[0], projected[1], projected[2])
    attended = head_norm(outputs).reshape(total_rows, HEADS * HEAD_DIM).astype(jnp.bfloat16)
    out_proj = lax.dot_general(attended, attn_weight[3], (((1,), (1,)), ((), ())), preferred_element_type=jnp.float32)
    residual = (tokens.astype(jnp.float32) + out_proj).astype(jnp.bfloat16)
    moe_in = rms_scale(residual, moe_gain).astype(jnp.bfloat16)
    route_rows = routes.reshape(N_SEQ, TOK_DEV * TOPK)
    slots = slot_numbers(route_rows)
    token_ids = jnp.repeat(jnp.arange(total_rows, dtype=jnp.int32).reshape(N_SEQ, TOK_DEV), TOPK, axis=1)
    block_ids = jnp.broadcast_to(jnp.arange(N_SEQ, dtype=jnp.int32)[:, None], slots.shape)
    owner_table = jnp.full((N_SEQ, EXPERTS * CAP), total_rows, jnp.int32).at[block_ids, slots].set(token_ids)
    weight_table = jnp.zeros((N_SEQ, EXPERTS * CAP), jnp.float32).at[block_ids, slots].set(gates.reshape(N_SEQ, TOK_DEV * TOPK))
    padded_in = jnp.concatenate([moe_in, jnp.zeros((1, D), jnp.bfloat16)], axis=0)

    def one_expert(moe_sum, expert_id):
        picked = lax.dynamic_slice_in_dim(owner_table, expert_id * CAP, CAP, 1).reshape(-1)
        slot_gate = lax.dynamic_slice_in_dim(weight_table, expert_id * CAP, CAP, 1).reshape(-1)
        produced = expert_apply(padded_in[picked], expert_gate[expert_id], expert_up[expert_id], expert_down[expert_id])
        return (moe_sum.at[picked].add(slot_gate[:, None] * produced), None)
    start_sum = jnp.zeros((total_rows + 1, D), jnp.float32)
    moe_sum, unused = lax.scan(one_expert, start_sum, jnp.arange(EXPERTS, dtype=jnp.int32))
    return (residual.astype(jnp.float32) + moe_sum[:total_rows]).astype(jnp.bfloat16)
```

```python
import functools

import jax
import jax.numpy as jnp
from jax import lax
from jax.experimental import pallas as pl
from jax.experimental.pallas import tpu as pltpu
from jax.sharding import PartitionSpec as P

HEAD_DIM = 128
EXPERTS = 64
TOPK = 8
CAP = 18
MESH = pl.DeviceIdType.MESH


PRECISE = lax.Precision.HIGHEST


def prefix_2(array, axis, combine, identity):
    peers, position = (lax.axis_size(axis), lax.axis_index(axis))
    everything = lax.all_gather(array.astype(jnp.bfloat16), axis)
    start = jnp.broadcast_to(jnp.asarray(identity, array.dtype), array.shape)

    def hop(k, before):
        reached = k < position
        new = combine(before, everything[k].astype(array.dtype))
        return jnp.where(reached, new, before)

    return lax.fori_loop(0, peers, hop, start)


def rms_scale(row_block, gain_vec):
    widened = row_block.astype(jnp.float32)
    factor = lax.rsqrt(jnp.mean(widened * widened, axis=-1, keepdims=True) + 1e-06)
    return widened * factor * gain_vec


def head_norm(outputs):
    return outputs * lax.rsqrt(jnp.mean(outputs * outputs, axis=-1, keepdims=True) + 1e-06)


def add_states(earlier, later):
    return earlier + later


def slot_numbers(route_flat):
    one_hot = (route_flat[:, None] == jnp.arange(EXPERTS, dtype=jnp.int32)[None, :]).astype(
        jnp.int32
    )
    earlier = jnp.cumsum(one_hot, axis=0) - one_hot
    return route_flat * CAP + jnp.sum(earlier * one_hot, axis=1)


def make_runner(expert_gate, expert_up, expert_down):

    def run_experts(received):
        gate_val = jnp.einsum(
            "necd,edf->necf", received, expert_gate, preferred_element_type=jnp.float32
        )
        up_val = jnp.einsum(
            "necd,edf->necf", received, expert_up, preferred_element_type=jnp.float32
        )
        hidden = (jax.nn.silu(gate_val) * up_val).astype(jnp.bfloat16)
        partial_value = jnp.einsum(
            "necf,efd->necd", hidden, expert_down, preferred_element_type=jnp.float32
        ).astype(jnp.bfloat16)
        groups = lax.axis_size("head")
        shape_now = partial_value.shape
        split = partial_value.reshape(
            shape_now[0], shape_now[1], shape_now[2], groups, shape_now[3] // groups
        )
        by_group = lax.all_to_all(split, "head", split_axis=3, concat_axis=3, tiled=True)
        summed = jnp.sum(by_group.astype(jnp.float32), axis=3)
        return lax.all_to_all(
            summed.astype(jnp.bfloat16), "seq", split_axis=0, concat_axis=0, tiled=True
        ).astype(summed.dtype)

    return run_experts


def body(
    tokens, attn_weight, attn_gain, moe_gain, routes, gates, expert_gate, expert_up, expert_down
):
    local_rows = tokens.shape[0]
    normed = rms_scale(tokens, attn_gain).astype(jnp.bfloat16)
    weights = lax.all_gather(attn_weight, "seq", axis=1, tiled=True)
    head_count = weights.shape[2] // HEAD_DIM
    projected = [
        jnp.dot(normed, weights[which], preferred_element_type=jnp.float32)
        .astype(jnp.bfloat16)
        .reshape(local_rows, head_count, HEAD_DIM)
        for which in range(3)
    ]
    query_rows, key_rows, value_rows = projected
    own_state = jnp.einsum("thd,the->hde", key_rows, value_rows, preferred_element_type=jnp.float32)
    prefix = prefix_2(own_state, "seq", add_states, jnp.zeros_like(own_state))
    inter_part = jnp.einsum(
        "thd,hde->the", query_rows.astype(jnp.float32), prefix, precision=PRECISE
    )
    scores = jnp.einsum("thd,shd->hts", query_rows, key_rows, preferred_element_type=jnp.float32)
    lower_mask = jnp.arange(local_rows)[:, None] >= jnp.arange(local_rows)[None, :]
    scores = jnp.where(lower_mask[None], scores, 0.0)
    intra_part = jnp.einsum(
        "hts,she->the", scores, value_rows.astype(jnp.float32), precision=PRECISE
    )
    attended = (
        head_norm(inter_part + intra_part)
        .reshape(local_rows, head_count * HEAD_DIM)
        .astype(jnp.bfloat16)
    )
    out_part = lax.dot_general(
        attended, weights[3], (((1,), (1,)), ((), ())), preferred_element_type=jnp.float32
    )
    residual = (
        tokens.astype(jnp.float32)
        + lax.psum(out_part.astype(jnp.bfloat16), "head").astype(jnp.float32)
    ).astype(jnp.bfloat16)
    moe_in = rms_scale(residual, moe_gain).astype(jnp.bfloat16)
    route_flat = routes.reshape(-1)
    slots = slot_numbers(route_flat)
    owners = lax.axis_size("seq")
    local_experts = expert_gate.shape[0]
    source_row = jnp.arange(route_flat.shape[0], dtype=jnp.int32) // TOPK
    run_experts = make_runner(expert_gate, expert_up, expert_down)
    outbound = (
        jnp.zeros((EXPERTS * CAP, moe_in.shape[1]), jnp.bfloat16).at[slots].set(moe_in[source_row])
    )
    outbound = outbound.reshape(owners, local_experts, CAP, moe_in.shape[1])
    returned = run_experts(lax.all_to_all(outbound, "seq", split_axis=0, concat_axis=0, tiled=True))
    arrived = returned.reshape(EXPERTS * CAP, -1)[slots].reshape(local_rows, TOPK, -1)
    moe_partial = jnp.einsum("tkd,tk->td", arrived, gates, precision=PRECISE)
    column_span = moe_partial.shape[1]
    residual_share = lax.dynamic_slice_in_dim(
        residual, lax.axis_index("head") * column_span, column_span, 1
    )
    mixed_share = (residual_share.astype(jnp.float32) + moe_partial).astype(jnp.bfloat16)
    return lax.all_gather(mixed_share, "head", axis=1, tiled=True)


def swap_kernel(axis, modes, *refs):
    count = len(modes)
    ins, outs = refs[:count], refs[count : 2 * count]
    send_sem, recv_sem, own_sem = refs[2 * count :]
    peers, me = lax.axis_size(axis), lax.axis_index(axis)
    barrier = pltpu.get_barrier_semaphore()
    for step in range(1, peers):
        pl.semaphore_signal(
            barrier, inc=1, device_id={axis: lax.rem(me + step, peers)}, device_id_type=MESH
        )
    pl.semaphore_wait(barrier, peers - 1)
    copies = []
    for step in range(1, peers):
        peer = lax.rem(me + step, peers)
        for which in range(count):
            source = ins[which].at[peer] if modes[which] else ins[which]
            copy = pltpu.make_async_remote_copy(
                src_ref=source,
                dst_ref=outs[which].at[me],
                send_sem=send_sem.at[which, step - 1],
                recv_sem=recv_sem.at[which, step - 1],
                device_id={axis: peer},
                device_id_type=MESH,
            )
            copy.start()
            copies.append(copy)
    own = []
    for which in range(count):
        source = ins[which].at[me] if modes[which] else ins[which]
        copy = pltpu.make_async_copy(source, outs[which].at[me], own_sem.at[which])
        copy.start()
        own.append(copy)
    for copy in own:
        copy.wait()
    for copy in copies:
        copy.wait()


def swap(arrays, modes, axis, ident):
    peers = lax.axis_size(axis)
    shapes = [
        jax.ShapeDtypeStruct(a.shape if mode else (peers,) + a.shape, a.dtype)
        for a, mode in zip(arrays, modes)
    ]
    spec = pl.BlockSpec(memory_space=pltpu.VMEM)
    return pl.pallas_call(
        functools.partial(swap_kernel, axis, tuple(modes)),
        out_shape=shapes,
        in_specs=[spec] * len(arrays),
        out_specs=[spec] * len(arrays),
        scratch_shapes=[
            pltpu.SemaphoreType.DMA((len(arrays), peers - 1)),
            pltpu.SemaphoreType.DMA((len(arrays), peers - 1)),
            pltpu.SemaphoreType.DMA((len(arrays),)),
        ],
        compiler_params=pltpu.CompilerParams(collective_id=ident, has_side_effects=True),
    )(*arrays)


def pair_of(me, bit):
    side = lax.rem(me // bit, 2)
    return side, me + bit * (1 - 2 * side)


def pair_barrier(peer, axis):
    barrier = pltpu.get_barrier_semaphore()
    pl.semaphore_signal(barrier, inc=1, device_id={axis: peer}, device_id_type=MESH)
    pl.semaphore_wait(barrier, 1)


def pair_gather_kernel(axis, bit, x_ref, o_ref, send_sem, recv_sem, own_sem):
    side, peer = pair_of(lax.axis_index(axis), bit)
    pair_barrier(peer, axis)
    copy = pltpu.make_async_remote_copy(
        src_ref=x_ref,
        dst_ref=o_ref.at[side],
        send_sem=send_sem,
        recv_sem=recv_sem,
        device_id={axis: peer},
        device_id_type=MESH,
    )
    copy.start()
    own = pltpu.make_async_copy(x_ref, o_ref.at[side], own_sem)
    own.start()
    own.wait()
    copy.wait()


def pair_sum_kernel(axis, bit, x_ref, o_ref, held, send_sem, recv_sem):
    side, peer = pair_of(lax.axis_index(axis), bit)
    pair_barrier(peer, axis)
    copy = pltpu.make_async_remote_copy(
        src_ref=x_ref.at[1 - side],
        dst_ref=held,
        send_sem=send_sem,
        recv_sem=recv_sem,
        device_id={axis: peer},
        device_id_type=MESH,
    )
    copy.start()
    copy.wait()
    for block in range(o_ref.shape[0]):
        o_ref[block] = (
            x_ref[side, block].astype(jnp.float32) + held[block].astype(jnp.float32)
        ).astype(o_ref.dtype)


def pair_call(kernel, x, axis, bit, shape, scratch, ident):
    spec = pl.BlockSpec(memory_space=pltpu.VMEM)
    return pl.pallas_call(
        functools.partial(kernel, axis, bit),
        out_shape=jax.ShapeDtypeStruct(shape, x.dtype),
        in_specs=[spec],
        out_specs=spec,
        scratch_shapes=scratch,
        compiler_params=pltpu.CompilerParams(collective_id=ident, has_side_effects=True),
    )(x)


def pair_gather(x, axis, bit, ident):
    sem = pltpu.SemaphoreType.DMA
    return pair_call(pair_gather_kernel, x, axis, bit, (2,) + x.shape, [sem, sem, sem], ident)


def pair_sum(x, axis, bit, ident):
    sem = pltpu.SemaphoreType.DMA
    shape = x.shape[1:]
    return pair_call(
        pair_sum_kernel, x, axis, bit, shape, [pltpu.VMEM(shape, x.dtype), sem, sem], ident
    )


def gather_bits(x, axis, ident):
    bits = lax.axis_size(axis).bit_length() - 1
    own = x.shape
    for k in reversed(range(bits)):
        x = pair_gather(x, axis, 1 << k, ident + k)
    x = x.transpose(tuple(reversed(range(bits))) + tuple(range(bits, x.ndim)))
    return x.reshape((lax.axis_size(axis),) + own)


def sum_bits(x, axis, ident):
    bits = lax.axis_size(axis).bit_length() - 1
    rest = x.shape[1:]
    for k in range(bits):
        left = x.shape[0] // 2
        x = x.reshape((left, 2) + rest).transpose((1, 0) + tuple(range(2, 2 + len(rest))))
        x = pair_sum(x, axis, 1 << k, ident + k)
    return x[0]


def moe_kernel(in_ref, pick_ref, mix_ref, gate_ref, up_ref, down_ref, o_ref, x_scr, y_scr):
    expert = pl.program_id(0)
    slots = x_scr.shape[0] // pl.num_programs(0)
    span = o_ref.shape[2]

    @pl.when(expert == 0)
    def _():
        for part in range(o_ref.shape[0]):
            x_scr[:, part * span : (part + 1) * span] = jnp.dot(
                pick_ref[...],
                in_ref[:, part * span : (part + 1) * span],
                preferred_element_type=jnp.float32,
            ).astype(jnp.bfloat16)

    rows = pl.ds(pl.multiple_of(expert * slots, slots), slots)
    x = x_scr[rows, :]
    gate_val = jnp.dot(x, gate_ref[0], preferred_element_type=jnp.float32)
    up_val = jnp.dot(x, up_ref[0], preferred_element_type=jnp.float32)
    hidden = (gate_val * jax.nn.sigmoid(gate_val) * up_val).astype(jnp.bfloat16)
    y_scr[rows, :] = jnp.dot(hidden, down_ref[0], preferred_element_type=jnp.float32).astype(
        jnp.bfloat16
    )

    @pl.when(expert == pl.num_programs(0) - 1)
    def _():
        for part in range(o_ref.shape[0]):
            o_ref[part] = jnp.dot(
                mix_ref[...],
                y_scr[:, part * span : (part + 1) * span],
                preferred_element_type=jnp.float32,
            ).astype(jnp.bfloat16)


def experts_here(moe_in, pick, mix, expert_gate, expert_up, expert_down, parts):
    amount, wide, inner = expert_gate.shape
    total = moe_in.shape[0]
    fixed = lambda e: (0, 0)
    one = lambda e: (e, 0, 0)
    return pl.pallas_call(
        moe_kernel,
        out_shape=jax.ShapeDtypeStruct((parts, total, wide // parts), jnp.bfloat16),
        grid=(amount,),
        in_specs=[
            pl.BlockSpec(moe_in.shape, fixed),
            pl.BlockSpec(pick.shape, fixed),
            pl.BlockSpec(mix.shape, fixed),
            pl.BlockSpec((1, wide, inner), one),
            pl.BlockSpec((1, wide, inner), one),
            pl.BlockSpec((1, inner, wide), one),
        ],
        out_specs=pl.BlockSpec((parts, total, wide // parts), lambda e: (0, 0, 0)),
        scratch_shapes=[
            pltpu.VMEM((pick.shape[0], wide), jnp.bfloat16),
            pltpu.VMEM((pick.shape[0], wide), jnp.bfloat16),
        ],
        compiler_params=pltpu.CompilerParams(dimension_semantics=("arbitrary",)),
    )(moe_in, pick, mix, expert_gate, expert_up, expert_down)


def slot_tables(route_rows, gate_rows, first, amount, slots):
    total = route_rows.shape[1]
    ids = (first + jnp.arange(amount)).astype(jnp.float32)
    hit = route_rows[None] == ids[:, None, None]
    named = jnp.any(hit, axis=1)
    weight = jnp.sum(jnp.where(hit, gate_rows[None], 0.0), axis=1)
    earlier = (jnp.arange(total)[:, None] < jnp.arange(total)[None, :]).astype(jnp.bfloat16)
    rank = jnp.dot(named.astype(jnp.bfloat16), earlier, preferred_element_type=jnp.float32)
    place = jnp.where(named, rank, -1.0)
    spots = jnp.arange(slots, dtype=jnp.float32)
    pick = (place[:, None, :] == spots[None, :, None]).astype(jnp.bfloat16)
    pick = pick.reshape(amount * slots, total)
    column = jnp.arange(amount * slots)
    spread = (column[None, :] // slots == jnp.arange(amount)[:, None]).astype(jnp.bfloat16)
    wide_place = lax.dot_general(
        place.astype(jnp.bfloat16), spread, (((0,), (0,)), ((), ())),
        preferred_element_type=jnp.float32,
    )
    wide_weight = lax.dot_general(
        weight.astype(jnp.bfloat16), spread, (((0,), (0,)), ((), ())),
        preferred_element_type=jnp.float32,
    )
    spot_of = (column % slots).astype(jnp.float32)
    mix = jnp.where(wide_place == spot_of[None, :], wide_weight, 0.0).astype(jnp.bfloat16)
    return pick, mix


def token_body(
    tokens, attn_weight, attn_gain, moe_gain, routes, gates, expert_gate, expert_up, expert_down
):
    local, width = tokens.shape
    n_seq, n_head = lax.axis_size("seq"), lax.axis_size("head")
    seq, head = lax.axis_index("seq"), lax.axis_index("head")
    total = n_seq * local
    depth, columns = attn_weight.shape[1:]
    own_cols = columns // n_seq
    wide_tokens = tokens.astype(jnp.float32)
    factor = lax.rsqrt(jnp.mean(wide_tokens * wide_tokens, axis=-1) + 1e-06)
    small = jnp.concatenate(
        [routes.T.astype(jnp.float32), gates.T, jnp.broadcast_to(factor[None], (8, local))]
    )
    pieces = tokens.reshape(local, n_seq, depth).transpose(1, 0, 2)
    piece_all, small_all = swap([pieces, small], [True, False], "seq", 1)
    mine = piece_all.reshape(total, depth)
    small_all = small_all.transpose(1, 0, 2).reshape(small.shape[0], total)
    gain = lax.dynamic_slice_in_dim(attn_gain, seq * depth, depth)
    normed = (
        mine.astype(jnp.float32) * small_all[2 * TOPK][:, None] * gain[None]
    ).astype(jnp.bfloat16)
    part = [
        jnp.dot(normed, attn_weight[which], preferred_element_type=jnp.float32)
        .astype(jnp.bfloat16)
        .reshape(total, n_seq, own_cols)
        for which in range(3)
    ]
    part = jnp.stack(part).transpose(2, 0, 1, 3)
    (part_all,) = swap([part], [True], "seq", 2)
    joined = jnp.sum(part_all.astype(jnp.float32), axis=0).astype(jnp.bfloat16)
    joined = joined.reshape(3, total, own_cols // HEAD_DIM, HEAD_DIM)
    scores = jnp.einsum("thd,shd->hts", joined[0], joined[1], preferred_element_type=jnp.float32)
    lower = jnp.arange(total)[:, None] >= jnp.arange(total)[None, :]
    scores = jnp.where(lower[None], scores, 0.0).astype(jnp.bfloat16)
    outputs = jnp.einsum("hts,she->the", scores, joined[2], preferred_element_type=jnp.float32)
    attended = head_norm(outputs).astype(jnp.bfloat16).reshape(total, own_cols)
    (attended_all,) = swap([attended], [False], "seq", 3)
    attended_all = attended_all.transpose(1, 0, 2).reshape(total, columns)
    out_part = lax.dot_general(
        attended_all, attn_weight[3], (((1,), (1,)), ((), ())), preferred_element_type=jnp.float32
    ).astype(jnp.bfloat16)
    rows = total // n_head
    out_sum = sum_bits(out_part.reshape(n_head, rows, depth), "head", 4)
    kept = lax.dynamic_slice_in_dim(mine, head * rows, rows, 0)
    residual_piece = (kept.astype(jnp.float32) + out_sum.astype(jnp.float32)).astype(jnp.bfloat16)
    (residual_rows,) = swap([residual_piece], [False], "seq", 8)
    residual = gather_bits(residual_rows, "head", 9)
    residual = residual.transpose(0, 2, 1, 3).reshape(total, width)
    moe_in = rms_scale(residual, moe_gain).astype(jnp.bfloat16)
    amount = expert_gate.shape[0]
    slots = -(-CAP * n_seq // 16) * 16
    pick, mix = slot_tables(
        small_all[:TOPK], small_all[TOPK : 2 * TOPK], seq * amount, amount, slots
    )
    sums = experts_here(moe_in, pick, mix, expert_gate, expert_up, expert_down, n_head)
    share = sum_bits(sums, "head", 13)
    (share_all,) = swap([share.reshape(n_seq, local, -1)], [True], "seq", 17)
    moe_out = jnp.sum(share_all.astype(jnp.float32), axis=0)
    span = moe_out.shape[1]
    own_rows = lax.dynamic_slice(residual, (seq * local, head * span), (local, span))
    mixed_share = (own_rows.astype(jnp.float32) + moe_out).astype(jnp.bfloat16)
    mixed = gather_bits(mixed_share, "head", 18)
    return mixed.transpose(1, 0, 2).reshape(local, width)


def solution(mesh):
    n_seq, n_head = mesh.shape["seq"], mesh.shape["head"]

    def run(tokens, attn_weight, *rest):
        heads_here = attn_weight.shape[2] // HEAD_DIM
        power = n_head & (n_head - 1) == 0 and n_head > 1
        if n_seq > 1 and power and heads_here % n_seq == 0:
            return token_body(tokens, attn_weight, *rest)
        return body(tokens, attn_weight, *rest)

    return jax.shard_map(
        run,
        mesh=mesh,
        in_specs=(
            P(("grp", "seq"), None),
            P(None, "seq", "head"),
            P(),
            P(),
            P(("grp", "seq"), None),
            P(("grp", "seq"), None),
            P("seq", None, "head"),
            P("seq", None, "head"),
            P("seq", "head", None),
        ),
        out_specs=P(("grp", "seq"), None),
        check_vma=False,
    )
```

```python
import functools

import jax
import jax.numpy as jnp
from jax import lax
from jax.experimental import pallas as pl
from jax.experimental.pallas import tpu as pltpu
from jax.sharding import PartitionSpec as P

HEAD_DIM = 128
EXPERTS = 64
TOPK = 8
CAP = 18
MESH = pl.DeviceIdType.MESH


PRECISE = lax.Precision.HIGHEST


def prefix_2(array, axis, combine, identity):
    peers, position = (lax.axis_size(axis), lax.axis_index(axis))
    everything = lax.all_gather(array.astype(jnp.bfloat16), axis)
    start = jnp.broadcast_to(jnp.asarray(identity, array.dtype), array.shape)

    def hop(k, before):
        reached = k < position
        new = combine(before, everything[k].astype(array.dtype))
        return jnp.where(reached, new, before)

    return lax.fori_loop(0, peers, hop, start)


def rms_scale(row_block, gain_vec):
    widened = row_block.astype(jnp.float32)
    factor = lax.rsqrt(jnp.mean(widened * widened, axis=-1, keepdims=True) + 1e-06)
    return widened * factor * gain_vec


def head_norm(outputs):
    return outputs * lax.rsqrt(jnp.mean(outputs * outputs, axis=-1, keepdims=True) + 1e-06)


def add_states(earlier, later):
    return earlier + later


def slot_numbers(route_flat):
    one_hot = (route_flat[:, None] == jnp.arange(EXPERTS, dtype=jnp.int32)[None, :]).astype(
        jnp.int32
    )
    earlier = jnp.cumsum(one_hot, axis=0) - one_hot
    return route_flat * CAP + jnp.sum(earlier * one_hot, axis=1)


def make_runner(expert_gate, expert_up, expert_down):

    def run_experts(received):
        gate_val = jnp.einsum(
            "necd,edf->necf", received, expert_gate, preferred_element_type=jnp.float32
        )
        up_val = jnp.einsum(
            "necd,edf->necf", received, expert_up, preferred_element_type=jnp.float32
        )
        hidden = (jax.nn.silu(gate_val) * up_val).astype(jnp.bfloat16)
        partial_value = jnp.einsum(
            "necf,efd->necd", hidden, expert_down, preferred_element_type=jnp.float32
        ).astype(jnp.bfloat16)
        groups = lax.axis_size("head")
        shape_now = partial_value.shape
        split = partial_value.reshape(
            shape_now[0], shape_now[1], shape_now[2], groups, shape_now[3] // groups
        )
        by_group = lax.all_to_all(split, "head", split_axis=3, concat_axis=3, tiled=True)
        summed = jnp.sum(by_group.astype(jnp.float32), axis=3)
        return lax.all_to_all(
            summed.astype(jnp.bfloat16), "seq", split_axis=0, concat_axis=0, tiled=True
        ).astype(summed.dtype)

    return run_experts


def body(
    tokens, attn_weight, attn_gain, moe_gain, routes, gates, expert_gate, expert_up, expert_down
):
    local_rows = tokens.shape[0]
    normed = rms_scale(tokens, attn_gain).astype(jnp.bfloat16)
    weights = lax.all_gather(attn_weight, "seq", axis=1, tiled=True)
    head_count = weights.shape[2] // HEAD_DIM
    projected = [
        jnp.dot(normed, weights[which], preferred_element_type=jnp.float32)
        .astype(jnp.bfloat16)
        .reshape(local_rows, head_count, HEAD_DIM)
        for which in range(3)
    ]
    query_rows, key_rows, value_rows = projected
    own_state = jnp.einsum("thd,the->hde", key_rows, value_rows, preferred_element_type=jnp.float32)
    prefix = prefix_2(own_state, "seq", add_states, jnp.zeros_like(own_state))
    inter_part = jnp.einsum(
        "thd,hde->the", query_rows.astype(jnp.float32), prefix, precision=PRECISE
    )
    scores = jnp.einsum("thd,shd->hts", query_rows, key_rows, preferred_element_type=jnp.float32)
    lower_mask = jnp.arange(local_rows)[:, None] >= jnp.arange(local_rows)[None, :]
    scores = jnp.where(lower_mask[None], scores, 0.0)
    intra_part = jnp.einsum(
        "hts,she->the", scores, value_rows.astype(jnp.float32), precision=PRECISE
    )
    attended = (
        head_norm(inter_part + intra_part)
        .reshape(local_rows, head_count * HEAD_DIM)
        .astype(jnp.bfloat16)
    )
    out_part = lax.dot_general(
        attended, weights[3], (((1,), (1,)), ((), ())), preferred_element_type=jnp.float32
    )
    residual = (
        tokens.astype(jnp.float32)
        + lax.psum(out_part.astype(jnp.bfloat16), "head").astype(jnp.float32)
    ).astype(jnp.bfloat16)
    moe_in = rms_scale(residual, moe_gain).astype(jnp.bfloat16)
    route_flat = routes.reshape(-1)
    slots = slot_numbers(route_flat)
    owners = lax.axis_size("seq")
    local_experts = expert_gate.shape[0]
    source_row = jnp.arange(route_flat.shape[0], dtype=jnp.int32) // TOPK
    run_experts = make_runner(expert_gate, expert_up, expert_down)
    outbound = (
        jnp.zeros((EXPERTS * CAP, moe_in.shape[1]), jnp.bfloat16).at[slots].set(moe_in[source_row])
    )
    outbound = outbound.reshape(owners, local_experts, CAP, moe_in.shape[1])
    returned = run_experts(lax.all_to_all(outbound, "seq", split_axis=0, concat_axis=0, tiled=True))
    arrived = returned.reshape(EXPERTS * CAP, -1)[slots].reshape(local_rows, TOPK, -1)
    moe_partial = jnp.einsum("tkd,tk->td", arrived, gates, precision=PRECISE)
    column_span = moe_partial.shape[1]
    residual_share = lax.dynamic_slice_in_dim(
        residual, lax.axis_index("head") * column_span, column_span, 1
    )
    mixed_share = (residual_share.astype(jnp.float32) + moe_partial).astype(jnp.bfloat16)
    return lax.all_gather(mixed_share, "head", axis=1, tiled=True)


def swap_kernel(axis, modes, *refs):
    count = len(modes)
    ins, outs = refs[:count], refs[count : 2 * count]
    send_sem, recv_sem, own_sem = refs[2 * count :]
    peers, me = lax.axis_size(axis), lax.axis_index(axis)
    barrier = pltpu.get_barrier_semaphore()
    for step in range(1, peers):
        pl.semaphore_signal(
            barrier, inc=1, device_id={axis: lax.rem(me + step, peers)}, device_id_type=MESH
        )
    pl.semaphore_wait(barrier, peers - 1)
    copies = []
    for step in range(1, peers):
        peer = lax.rem(me + step, peers)
        for which in range(count):
            source = ins[which].at[peer] if modes[which] else ins[which]
            copy = pltpu.make_async_remote_copy(
                src_ref=source,
                dst_ref=outs[which].at[me],
                send_sem=send_sem.at[which, step - 1],
                recv_sem=recv_sem.at[which, step - 1],
                device_id={axis: peer},
                device_id_type=MESH,
            )
            copy.start()
            copies.append(copy)
    own = []
    for which in range(count):
        source = ins[which].at[me] if modes[which] else ins[which]
        copy = pltpu.make_async_copy(source, outs[which].at[me], own_sem.at[which])
        copy.start()
        own.append(copy)
    for copy in own:
        copy.wait()
    for copy in copies:
        copy.wait()


def swap(arrays, modes, axis, ident):
    peers = lax.axis_size(axis)
    shapes = [
        jax.ShapeDtypeStruct(a.shape if mode else (peers,) + a.shape, a.dtype)
        for a, mode in zip(arrays, modes)
    ]
    spec = pl.BlockSpec(memory_space=pltpu.VMEM)
    return pl.pallas_call(
        functools.partial(swap_kernel, axis, tuple(modes)),
        out_shape=shapes,
        in_specs=[spec] * len(arrays),
        out_specs=[spec] * len(arrays),
        scratch_shapes=[
            pltpu.SemaphoreType.DMA((len(arrays), peers - 1)),
            pltpu.SemaphoreType.DMA((len(arrays), peers - 1)),
            pltpu.SemaphoreType.DMA((len(arrays),)),
        ],
        compiler_params=pltpu.CompilerParams(collective_id=ident, has_side_effects=True),
    )(*arrays)


def pair_of(me, bit):
    side = lax.rem(me // bit, 2)
    return side, me + bit * (1 - 2 * side)


def pair_barrier(peer, axis):
    barrier = pltpu.get_barrier_semaphore()
    pl.semaphore_signal(barrier, inc=1, device_id={axis: peer}, device_id_type=MESH)
    pl.semaphore_wait(barrier, 1)


def pair_sum_kernel(axis, bit, x_ref, o_ref, held, send_sem, recv_sem):
    side, peer = pair_of(lax.axis_index(axis), bit)
    pair_barrier(peer, axis)
    copy = pltpu.make_async_remote_copy(
        src_ref=x_ref.at[1 - side],
        dst_ref=held,
        send_sem=send_sem,
        recv_sem=recv_sem,
        device_id={axis: peer},
        device_id_type=MESH,
    )
    copy.start()
    copy.wait()
    for block in range(o_ref.shape[0]):
        o_ref[block] = (
            x_ref[side, block].astype(jnp.float32) + held[block].astype(jnp.float32)
        ).astype(o_ref.dtype)


def pair_call(kernel, x, axis, bit, shape, scratch, ident):
    spec = pl.BlockSpec(memory_space=pltpu.VMEM)
    return pl.pallas_call(
        functools.partial(kernel, axis, bit),
        out_shape=jax.ShapeDtypeStruct(shape, x.dtype),
        in_specs=[spec],
        out_specs=spec,
        scratch_shapes=scratch,
        compiler_params=pltpu.CompilerParams(collective_id=ident, has_side_effects=True),
    )(x)


def pair_sum(x, axis, bit, ident):
    sem = pltpu.SemaphoreType.DMA
    shape = x.shape[1:]
    return pair_call(
        pair_sum_kernel, x, axis, bit, shape, [pltpu.VMEM(shape, x.dtype), sem, sem], ident
    )


def flip(index, bit):
    return index + bit * (1 - 2 * lax.rem(index // bit, 2))


def masked(index, mask):
    bit = 1
    while bit <= mask:
        if mask & bit:
            index = flip(index, bit)
        bit *= 2
    return index


def below(mask, peers):
    bits = [1 << k for k in reversed(range(peers.bit_length() - 1))]
    return [bit for bit in bits if mask == 0 or bit < (mask & -mask)]


def arrivals(peers):
    order = [0]
    for mask in order:
        order.extend(mask + bit for bit in below(mask, peers))
    return order


def greet(axis_peers):
    barrier = pltpu.get_barrier_semaphore()
    for target in axis_peers:
        pl.semaphore_signal(barrier, inc=1, device_id=target, device_id_type=MESH)
    pl.semaphore_wait(barrier, len(axis_peers))


def remote(source, dest, send_sem, recv_sem, target):
    return pltpu.make_async_remote_copy(
        src_ref=source,
        dst_ref=dest,
        send_sem=send_sem,
        recv_sem=recv_sem,
        device_id=target,
        device_id_type=MESH,
    )


def spread_kernel(split, x_ref, o_ref, send_sem, recv_sem, own_sem):
    n_seq, n_head = lax.axis_size("seq"), lax.axis_size("head")
    seq, head = lax.axis_index("seq"), lax.axis_index("head")
    rows, cols = x_ref.shape[-2:]
    bits = [1 << k for k in range(n_head.bit_length() - 1)]

    def place(head_at, seq_at):
        if split:
            return o_ref.at[seq_at, head_at]
        return o_ref.at[
            pl.ds(pl.multiple_of(head_at * rows, rows), rows),
            pl.ds(pl.multiple_of(seq_at * cols, cols), cols),
        ]

    peers = [{"seq": lax.rem(seq + k, n_seq)} for k in range(1, n_seq)]
    greet(peers + [{"head": flip(head, bit)} for bit in bits])
    copies = {}
    for k in range(1, n_seq):
        to = lax.rem(seq + k, n_seq)
        copies[0, k] = remote(
            x_ref.at[to, head] if split else x_ref,
            place(head, seq),
            send_sem.at[0, k],
            recv_sem.at[0, k],
            {"seq": to},
        )
        copies[0, k].start()
    if split:
        own = pltpu.make_async_copy(x_ref.at[seq], o_ref.at[seq], own_sem)
    else:
        own = pltpu.make_async_copy(x_ref, place(head, seq), own_sem)
    own.start()
    for mask in arrivals(n_head):
        for k in range(1 if split else 0, n_seq):
            if (mask, k) in copies:
                copies[mask, k].wait_recv()
            block = place(masked(head, mask), lax.rem(seq + n_seq - k, n_seq))
            source = x_ref if (mask, k) == (0, 0) else block
            for bit in below(mask, n_head):
                copy = remote(
                    source,
                    block,
                    send_sem.at[mask + bit, k],
                    recv_sem.at[mask + bit, k],
                    {"head": flip(head, bit)},
                )
                copy.start()
                copies[mask + bit, k] = copy
    own.wait()
    for copy in copies.values():
        copy.wait_send()


def spread(x, split, ident):
    n_seq, n_head = lax.axis_size("seq"), lax.axis_size("head")
    rows, cols = x.shape[-2:]
    shape = x.shape if split else (n_head * rows, n_seq * cols)
    sem = pltpu.SemaphoreType.DMA
    spec = pl.BlockSpec(memory_space=pltpu.VMEM)
    return pl.pallas_call(
        functools.partial(spread_kernel, split),
        out_shape=jax.ShapeDtypeStruct(shape, x.dtype),
        in_specs=[spec],
        out_specs=spec,
        scratch_shapes=[sem((n_head, n_seq)), sem((n_head, n_seq)), sem],
        compiler_params=pltpu.CompilerParams(collective_id=ident, has_side_effects=True),
    )(x)


def finish_kernel(
    x_ref, keep_ref, o_ref, held, buf, got, share, pair_sems, seq_sems, head_sems, own_sem
):
    n_seq, n_head = lax.axis_size("seq"), lax.axis_size("head")
    seq, head = lax.axis_index("seq"), lax.axis_index("head")
    top = n_head // 2
    side, peer = head // top, flip(head, top)
    span = share.shape[1]
    bits = [1 << k for k in range(n_head.bit_length() - 1)]
    peers = [{"seq": lax.rem(seq + k, n_seq)} for k in range(1, n_seq)]
    greet(peers + [{"head": flip(head, bit)} for bit in bits])
    order = list(range(1, n_seq)) + [0]
    firsts, swaps = {}, {}
    for k in order:
        to = lax.rem(seq + k, n_seq)
        firsts[k] = remote(
            x_ref.at[1 - side, to], held.at[k], pair_sems.at[0, k], pair_sems.at[1, k],
            {"head": peer},
        )
        firsts[k].start()
    for k in order:
        to = lax.rem(seq + k, n_seq)
        firsts[k].wait_recv()
        value = x_ref[side, to].astype(jnp.float32) + held[k].astype(jnp.float32)
        if k:
            buf[k] = value.astype(buf.dtype)
            swaps[k] = remote(
                buf.at[k], got.at[k], seq_sems.at[0, k], seq_sems.at[1, k], {"seq": to}
            )
            swaps[k].start()
        else:
            total = value + keep_ref[...].astype(jnp.float32)
    for k in range(1, n_seq):
        swaps[k].wait_recv()
        total = total + got[k].astype(jnp.float32)
    share[...] = total.astype(share.dtype)

    def place(head_at):
        return o_ref.at[:, pl.ds(pl.multiple_of(head_at * span, span), span)]

    copies = {}
    for mask in arrivals(n_head):
        if mask in copies:
            copies[mask].wait_recv()
        block = place(masked(head, mask))
        for bit in below(mask, n_head):
            copies[mask + bit] = remote(
                block if mask else share,
                block,
                head_sems.at[0, mask + bit],
                head_sems.at[1, mask + bit],
                {"head": flip(head, bit)},
            )
            copies[mask + bit].start()
    own = pltpu.make_async_copy(share, place(head), own_sem)
    own.start()
    own.wait()
    for copy in (*firsts.values(), *swaps.values(), *copies.values()):
        copy.wait_send()


def finish(sums, keep, ident):
    n_seq, n_head = lax.axis_size("seq"), lax.axis_size("head")
    local, span = keep.shape
    sem = pltpu.SemaphoreType.DMA
    spec = pl.BlockSpec(memory_space=pltpu.VMEM)
    blocks = pltpu.VMEM((n_seq, local, span), sums.dtype)
    return pl.pallas_call(
        finish_kernel,
        out_shape=jax.ShapeDtypeStruct((local, n_head * span), keep.dtype),
        in_specs=[spec] * 2,
        out_specs=spec,
        scratch_shapes=[
            blocks,
            blocks,
            blocks,
            pltpu.VMEM((local, span), keep.dtype),
            sem((2, n_seq)),
            sem((2, n_seq)),
            sem((2, n_head)),
            sem,
        ],
        compiler_params=pltpu.CompilerParams(collective_id=ident, has_side_effects=True),
    )(sums, keep)


def sum_bits(x, axis, bits, ident):
    for k in range(bits):
        x = pair_sum(x.reshape((2, -1) + x.shape[-2:]), axis, 1 << k, ident + k)
    return x


def low_first(index, bits):
    return sum(((index >> k) & 1) << (bits - 1 - k) for k in range(bits))


def moe_kernel(in_ref, pick_ref, mix_ref, gate_ref, up_ref, down_ref, o_ref, x_scr, y_scr):
    expert = pl.program_id(0)
    slots = x_scr.shape[0] // pl.num_programs(0)
    span = o_ref.shape[2]

    @pl.when(expert == 0)
    def _():
        for part in range(o_ref.shape[0]):
            x_scr[:, part * span : (part + 1) * span] = jnp.dot(
                pick_ref[...],
                in_ref[:, part * span : (part + 1) * span],
                preferred_element_type=jnp.float32,
            ).astype(jnp.bfloat16)

    rows = pl.ds(pl.multiple_of(expert * slots, slots), slots)
    x = x_scr[rows, :]
    gate_val = jnp.dot(x, gate_ref[0], preferred_element_type=jnp.float32)
    up_val = jnp.dot(x, up_ref[0], preferred_element_type=jnp.float32)
    hidden = (gate_val * jax.nn.sigmoid(gate_val) * up_val).astype(jnp.bfloat16)
    y_scr[rows, :] = jnp.dot(hidden, down_ref[0], preferred_element_type=jnp.float32).astype(
        jnp.bfloat16
    )

    @pl.when(expert == pl.num_programs(0) - 1)
    def _():
        for part in range(o_ref.shape[0]):
            bits = o_ref.shape[0].bit_length() - 1
            o_ref[low_first(part, bits)] = jnp.dot(
                mix_ref[...],
                y_scr[:, part * span : (part + 1) * span],
                preferred_element_type=jnp.float32,
            ).astype(jnp.bfloat16)


def experts_here(moe_in, pick, mix, expert_gate, expert_up, expert_down, parts):
    amount, wide, inner = expert_gate.shape
    total = moe_in.shape[0]
    fixed = lambda e: (0, 0)
    one = lambda e: (e, 0, 0)
    return pl.pallas_call(
        moe_kernel,
        out_shape=jax.ShapeDtypeStruct((parts, total, wide // parts), jnp.bfloat16),
        grid=(amount,),
        in_specs=[
            pl.BlockSpec(moe_in.shape, fixed),
            pl.BlockSpec(pick.shape, fixed),
            pl.BlockSpec(mix.shape, fixed),
            pl.BlockSpec((1, wide, inner), one),
            pl.BlockSpec((1, wide, inner), one),
            pl.BlockSpec((1, inner, wide), one),
        ],
        out_specs=pl.BlockSpec((parts, total, wide // parts), lambda e: (0, 0, 0)),
        scratch_shapes=[
            pltpu.VMEM((pick.shape[0], wide), jnp.bfloat16),
            pltpu.VMEM((pick.shape[0], wide), jnp.bfloat16),
        ],
        compiler_params=pltpu.CompilerParams(dimension_semantics=("arbitrary",)),
    )(moe_in, pick, mix, expert_gate, expert_up, expert_down)


def slot_tables(route_rows, gate_rows, first, amount, slots):
    total = route_rows.shape[1]
    ids = (first + jnp.arange(amount)).astype(jnp.float32)
    hit = route_rows[None] == ids[:, None, None]
    named = jnp.any(hit, axis=1)
    weight = jnp.sum(jnp.where(hit, gate_rows[None], 0.0), axis=1)
    earlier = (jnp.arange(total)[:, None] < jnp.arange(total)[None, :]).astype(jnp.bfloat16)
    rank = jnp.dot(named.astype(jnp.bfloat16), earlier, preferred_element_type=jnp.float32)
    place = jnp.where(named, rank, -1.0)
    spots = jnp.arange(slots, dtype=jnp.float32)
    pick = (place[:, None, :] == spots[None, :, None]).astype(jnp.bfloat16)
    pick = pick.reshape(amount * slots, total)
    column = jnp.arange(amount * slots)
    spread = (column[None, :] // slots == jnp.arange(amount)[:, None]).astype(jnp.bfloat16)
    wide_place = lax.dot_general(
        place.astype(jnp.bfloat16), spread, (((0,), (0,)), ((), ())),
        preferred_element_type=jnp.float32,
    )
    wide_weight = lax.dot_general(
        weight.astype(jnp.bfloat16), spread, (((0,), (0,)), ((), ())),
        preferred_element_type=jnp.float32,
    )
    spot_of = (column % slots).astype(jnp.float32)
    mix = jnp.where(wide_place == spot_of[None, :], wide_weight, 0.0).astype(jnp.bfloat16)
    return pick, mix


def token_body(
    tokens, attn_weight, attn_gain, moe_gain, routes, gates, expert_gate, expert_up, expert_down
):
    local, width = tokens.shape
    n_seq, n_head = lax.axis_size("seq"), lax.axis_size("head")
    seq, head = lax.axis_index("seq"), lax.axis_index("head")
    total = n_seq * local
    depth, columns = attn_weight.shape[1:]
    own_cols = columns // n_seq
    wide_tokens = tokens.astype(jnp.float32)
    factor = lax.rsqrt(jnp.mean(wide_tokens * wide_tokens, axis=-1) + 1e-06)
    small = jnp.concatenate(
        [routes.T.astype(jnp.float32), gates.T, jnp.broadcast_to(factor[None], (8, local))]
    )
    pieces = tokens.reshape(n_head, local // n_head, n_seq, depth).transpose(2, 0, 1, 3)
    (small_all,) = swap([small], [False], "seq", 1)
    mine = spread(pieces, True, 2).reshape(total, depth)
    small_all = small_all.transpose(1, 0, 2).reshape(small.shape[0], total)
    gain = lax.dynamic_slice_in_dim(attn_gain, seq * depth, depth)
    normed = (
        mine.astype(jnp.float32) * small_all[2 * TOPK][:, None] * gain[None]
    ).astype(jnp.bfloat16)
    part = [
        jnp.dot(normed, attn_weight[which], preferred_element_type=jnp.float32)
        .astype(jnp.bfloat16)
        .reshape(total, n_seq, own_cols)
        for which in range(3)
    ]
    part = jnp.stack(part).transpose(2, 0, 1, 3)
    (part_all,) = swap([part], [True], "seq", 3)
    joined = jnp.sum(part_all.astype(jnp.float32), axis=0).astype(jnp.bfloat16)
    joined = joined.reshape(3, total, own_cols // HEAD_DIM, HEAD_DIM)
    scores = jnp.einsum("thd,shd->hts", joined[0], joined[1], preferred_element_type=jnp.float32)
    lower = jnp.arange(total)[:, None] >= jnp.arange(total)[None, :]
    scores = jnp.where(lower[None], scores, 0.0).astype(jnp.bfloat16)
    outputs = jnp.einsum("hts,she->the", scores, joined[2], preferred_element_type=jnp.float32)
    attended = head_norm(outputs).astype(jnp.bfloat16).reshape(total, own_cols)
    (attended_all,) = swap([attended], [False], "seq", 4)
    attended_all = attended_all.transpose(1, 0, 2).reshape(total, columns)
    out_part = lax.dot_general(
        attended_all, attn_weight[3], (((1,), (1,)), ((), ())), preferred_element_type=jnp.float32
    ).astype(jnp.bfloat16)
    rows = total // n_head
    bits = n_head.bit_length() - 1
    out_part = jnp.stack(
        [out_part[low_first(k, bits) * rows : (low_first(k, bits) + 1) * rows] for k in range(n_head)]
    )
    out_sum = sum_bits(out_part, "head", bits, 5).reshape(rows, depth)
    kept = lax.dynamic_slice_in_dim(mine, head * rows, rows, 0)
    residual_piece = (kept.astype(jnp.float32) + out_sum.astype(jnp.float32)).astype(jnp.bfloat16)
    residual = spread(residual_piece, False, 5 + bits)
    moe_in = rms_scale(residual, moe_gain).astype(jnp.bfloat16)
    amount = expert_gate.shape[0]
    slots = -(-CAP * n_seq // 16) * 16
    pick, mix = slot_tables(
        small_all[:TOPK], small_all[TOPK : 2 * TOPK], seq * amount, amount, slots
    )
    sums = experts_here(moe_in, pick, mix, expert_gate, expert_up, expert_down, n_head)
    span = width // n_head
    pair = sum_bits(sums, "head", bits - 1, 6 + bits).reshape(2, n_seq, local, span)
    own_rows = lax.dynamic_slice(residual, (seq * local, head * span), (local, span))
    return finish(pair, own_rows, 6 + 2 * bits)


def solution(mesh):
    n_seq, n_head = mesh.shape["seq"], mesh.shape["head"]

    def run(tokens, attn_weight, *rest):
        heads_here = attn_weight.shape[2] // HEAD_DIM
        power = n_head & (n_head - 1) == 0 and n_head > 1
        if n_seq > 1 and power and heads_here % n_seq == 0:
            return token_body(tokens, attn_weight, *rest)
        return body(tokens, attn_weight, *rest)

    return jax.shard_map(
        run,
        mesh=mesh,
        in_specs=(
            P(("grp", "seq"), None),
            P(None, "seq", "head"),
            P(),
            P(),
            P(("grp", "seq"), None),
            P(("grp", "seq"), None),
            P("seq", None, "head"),
            P("seq", None, "head"),
            P("seq", "head", None),
        ),
        out_specs=P(("grp", "seq"), None),
        check_vma=False,
    )
```

```python
import functools

import jax
import jax.numpy as jnp
from jax import lax
from jax.experimental import pallas as pl
from jax.experimental.pallas import tpu as pltpu
from jax.sharding import PartitionSpec as P

HEAD_DIM = 128
EXPERTS = 64
TOPK = 8
CAP = 18
MESH = pl.DeviceIdType.MESH


PRECISE = lax.Precision.HIGHEST


def prefix_2(array, axis, combine, identity):
    peers, position = (lax.axis_size(axis), lax.axis_index(axis))
    everything = lax.all_gather(array.astype(jnp.bfloat16), axis)
    start = jnp.broadcast_to(jnp.asarray(identity, array.dtype), array.shape)

    def hop(k, before):
        reached = k < position
        new = combine(before, everything[k].astype(array.dtype))
        return jnp.where(reached, new, before)

    return lax.fori_loop(0, peers, hop, start)


def rms_scale(row_block, gain_vec):
    widened = row_block.astype(jnp.float32)
    factor = lax.rsqrt(jnp.mean(widened * widened, axis=-1, keepdims=True) + 1e-06)
    return widened * factor * gain_vec


def head_norm(outputs):
    return outputs * lax.rsqrt(jnp.mean(outputs * outputs, axis=-1, keepdims=True) + 1e-06)


def add_states(earlier, later):
    return earlier + later


def slot_numbers(route_flat):
    one_hot = (route_flat[:, None] == jnp.arange(EXPERTS, dtype=jnp.int32)[None, :]).astype(
        jnp.int32
    )
    earlier = jnp.cumsum(one_hot, axis=0) - one_hot
    return route_flat * CAP + jnp.sum(earlier * one_hot, axis=1)


def make_runner(expert_gate, expert_up, expert_down):

    def run_experts(received):
        gate_val = jnp.einsum(
            "necd,edf->necf", received, expert_gate, preferred_element_type=jnp.float32
        )
        up_val = jnp.einsum(
            "necd,edf->necf", received, expert_up, preferred_element_type=jnp.float32
        )
        hidden = (jax.nn.silu(gate_val) * up_val).astype(jnp.bfloat16)
        partial_value = jnp.einsum(
            "necf,efd->necd", hidden, expert_down, preferred_element_type=jnp.float32
        ).astype(jnp.bfloat16)
        groups = lax.axis_size("head")
        shape_now = partial_value.shape
        split = partial_value.reshape(
            shape_now[0], shape_now[1], shape_now[2], groups, shape_now[3] // groups
        )
        by_group = lax.all_to_all(split, "head", split_axis=3, concat_axis=3, tiled=True)
        summed = jnp.sum(by_group.astype(jnp.float32), axis=3)
        return lax.all_to_all(
            summed.astype(jnp.bfloat16), "seq", split_axis=0, concat_axis=0, tiled=True
        ).astype(summed.dtype)

    return run_experts


def body(
    tokens, attn_weight, attn_gain, moe_gain, routes, gates, expert_gate, expert_up, expert_down
):
    local_rows = tokens.shape[0]
    normed = rms_scale(tokens, attn_gain).astype(jnp.bfloat16)
    weights = lax.all_gather(attn_weight, "seq", axis=1, tiled=True)
    head_count = weights.shape[2] // HEAD_DIM
    projected = [
        jnp.dot(normed, weights[which], preferred_element_type=jnp.float32)
        .astype(jnp.bfloat16)
        .reshape(local_rows, head_count, HEAD_DIM)
        for which in range(3)
    ]
    query_rows, key_rows, value_rows = projected
    own_state = jnp.einsum("thd,the->hde", key_rows, value_rows, preferred_element_type=jnp.float32)
    prefix = prefix_2(own_state, "seq", add_states, jnp.zeros_like(own_state))
    inter_part = jnp.einsum(
        "thd,hde->the", query_rows.astype(jnp.float32), prefix, precision=PRECISE
    )
    scores = jnp.einsum("thd,shd->hts", query_rows, key_rows, preferred_element_type=jnp.float32)
    lower_mask = jnp.arange(local_rows)[:, None] >= jnp.arange(local_rows)[None, :]
    scores = jnp.where(lower_mask[None], scores, 0.0)
    intra_part = jnp.einsum(
        "hts,she->the", scores, value_rows.astype(jnp.float32), precision=PRECISE
    )
    attended = (
        head_norm(inter_part + intra_part)
        .reshape(local_rows, head_count * HEAD_DIM)
        .astype(jnp.bfloat16)
    )
    out_part = lax.dot_general(
        attended, weights[3], (((1,), (1,)), ((), ())), preferred_element_type=jnp.float32
    )
    residual = (
        tokens.astype(jnp.float32)
        + lax.psum(out_part.astype(jnp.bfloat16), "head").astype(jnp.float32)
    ).astype(jnp.bfloat16)
    moe_in = rms_scale(residual, moe_gain).astype(jnp.bfloat16)
    route_flat = routes.reshape(-1)
    slots = slot_numbers(route_flat)
    owners = lax.axis_size("seq")
    local_experts = expert_gate.shape[0]
    source_row = jnp.arange(route_flat.shape[0], dtype=jnp.int32) // TOPK
    run_experts = make_runner(expert_gate, expert_up, expert_down)
    outbound = (
        jnp.zeros((EXPERTS * CAP, moe_in.shape[1]), jnp.bfloat16).at[slots].set(moe_in[source_row])
    )
    outbound = outbound.reshape(owners, local_experts, CAP, moe_in.shape[1])
    returned = run_experts(lax.all_to_all(outbound, "seq", split_axis=0, concat_axis=0, tiled=True))
    arrived = returned.reshape(EXPERTS * CAP, -1)[slots].reshape(local_rows, TOPK, -1)
    moe_partial = jnp.einsum("tkd,tk->td", arrived, gates, precision=PRECISE)
    column_span = moe_partial.shape[1]
    residual_share = lax.dynamic_slice_in_dim(
        residual, lax.axis_index("head") * column_span, column_span, 1
    )
    mixed_share = (residual_share.astype(jnp.float32) + moe_partial).astype(jnp.bfloat16)
    return lax.all_gather(mixed_share, "head", axis=1, tiled=True)


def swap_kernel(axis, modes, *refs):
    count = len(modes)
    ins, outs = refs[:count], refs[count : 2 * count]
    send_sem, recv_sem, own_sem = refs[2 * count :]
    peers, me = lax.axis_size(axis), lax.axis_index(axis)
    barrier = pltpu.get_barrier_semaphore()
    for step in range(1, peers):
        pl.semaphore_signal(
            barrier, inc=1, device_id={axis: lax.rem(me + step, peers)}, device_id_type=MESH
        )
    pl.semaphore_wait(barrier, peers - 1)
    copies = []
    for step in range(1, peers):
        peer = lax.rem(me + step, peers)
        for which in range(count):
            source = ins[which].at[peer] if modes[which] else ins[which]
            copy = pltpu.make_async_remote_copy(
                src_ref=source,
                dst_ref=outs[which].at[me],
                send_sem=send_sem.at[which, step - 1],
                recv_sem=recv_sem.at[which, step - 1],
                device_id={axis: peer},
                device_id_type=MESH,
            )
            copy.start()
            copies.append(copy)
    own = []
    for which in range(count):
        source = ins[which].at[me] if modes[which] else ins[which]
        copy = pltpu.make_async_copy(source, outs[which].at[me], own_sem.at[which])
        copy.start()
        own.append(copy)
    for copy in own:
        copy.wait()
    for copy in copies:
        copy.wait()


def swap(arrays, modes, axis, ident):
    peers = lax.axis_size(axis)
    shapes = [
        jax.ShapeDtypeStruct(a.shape if mode else (peers,) + a.shape, a.dtype)
        for a, mode in zip(arrays, modes)
    ]
    spec = pl.BlockSpec(memory_space=pltpu.VMEM)
    return pl.pallas_call(
        functools.partial(swap_kernel, axis, tuple(modes)),
        out_shape=shapes,
        in_specs=[spec] * len(arrays),
        out_specs=[spec] * len(arrays),
        scratch_shapes=[
            pltpu.SemaphoreType.DMA((len(arrays), peers - 1)),
            pltpu.SemaphoreType.DMA((len(arrays), peers - 1)),
            pltpu.SemaphoreType.DMA((len(arrays),)),
        ],
        compiler_params=pltpu.CompilerParams(collective_id=ident, has_side_effects=True),
    )(*arrays)


def pair_of(me, bit):
    side = lax.rem(me // bit, 2)
    return side, me + bit * (1 - 2 * side)


def pair_barrier(peer, axis):
    barrier = pltpu.get_barrier_semaphore()
    pl.semaphore_signal(barrier, inc=1, device_id={axis: peer}, device_id_type=MESH)
    pl.semaphore_wait(barrier, 1)


def pair_sum_kernel(axis, bit, x_ref, o_ref, held, send_sem, recv_sem):
    side, peer = pair_of(lax.axis_index(axis), bit)
    pair_barrier(peer, axis)
    copy = pltpu.make_async_remote_copy(
        src_ref=x_ref.at[1 - side],
        dst_ref=held,
        send_sem=send_sem,
        recv_sem=recv_sem,
        device_id={axis: peer},
        device_id_type=MESH,
    )
    copy.start()
    copy.wait()
    for block in range(o_ref.shape[0]):
        o_ref[block] = (
            x_ref[side, block].astype(jnp.float32) + held[block].astype(jnp.float32)
        ).astype(o_ref.dtype)


def pair_call(kernel, x, axis, bit, shape, scratch, ident):
    spec = pl.BlockSpec(memory_space=pltpu.VMEM)
    return pl.pallas_call(
        functools.partial(kernel, axis, bit),
        out_shape=jax.ShapeDtypeStruct(shape, x.dtype),
        in_specs=[spec],
        out_specs=spec,
        scratch_shapes=scratch,
        compiler_params=pltpu.CompilerParams(collective_id=ident, has_side_effects=True),
    )(x)


def pair_sum(x, axis, bit, ident):
    sem = pltpu.SemaphoreType.DMA
    shape = x.shape[1:]
    return pair_call(
        pair_sum_kernel, x, axis, bit, shape, [pltpu.VMEM(shape, x.dtype), sem, sem], ident
    )


def flip(index, bit):
    return index + bit * (1 - 2 * lax.rem(index // bit, 2))


def masked(index, mask):
    bit = 1
    while bit <= mask:
        if mask & bit:
            index = flip(index, bit)
        bit *= 2
    return index


def below(mask, peers):
    bits = [1 << k for k in reversed(range(peers.bit_length() - 1))]
    return [bit for bit in bits if mask == 0 or bit < (mask & -mask)]


def arrivals(peers):
    order = [0]
    for mask in order:
        order.extend(mask + bit for bit in below(mask, peers))
    return order


def greet(axis_peers):
    barrier = pltpu.get_barrier_semaphore()
    for target in axis_peers:
        pl.semaphore_signal(barrier, inc=1, device_id=target, device_id_type=MESH)
    pl.semaphore_wait(barrier, len(axis_peers))


def remote(source, dest, send_sem, recv_sem, target):
    return pltpu.make_async_remote_copy(
        src_ref=source,
        dst_ref=dest,
        send_sem=send_sem,
        recv_sem=recv_sem,
        device_id=target,
        device_id_type=MESH,
    )


def spread_kernel(split, *refs):
    if split:
        x_ref, t_ref, o_ref, to_ref, send_sem, recv_sem, own_sem, t_sems = refs
    else:
        x_ref, o_ref, send_sem, recv_sem, own_sem = refs
    n_seq, n_head = lax.axis_size("seq"), lax.axis_size("head")
    seq, head = lax.axis_index("seq"), lax.axis_index("head")
    rows, cols = x_ref.shape[-2:]
    bits = [1 << k for k in range(n_head.bit_length() - 1)]

    def place(head_at, seq_at):
        if split:
            return o_ref.at[seq_at, head_at]
        return o_ref.at[
            pl.ds(pl.multiple_of(head_at * rows, rows), rows),
            pl.ds(pl.multiple_of(seq_at * cols, cols), cols),
        ]

    peers = [{"seq": lax.rem(seq + k, n_seq)} for k in range(1, n_seq)]
    greet(peers + [{"head": flip(head, bit)} for bit in bits])
    copies, tables = {}, []
    for k in range(1, n_seq):
        to = lax.rem(seq + k, n_seq)
        if split:
            tables.append(
                remote(t_ref, to_ref.at[seq], t_sems.at[0, k], t_sems.at[1, k], {"seq": to})
            )
            tables[-1].start()
        copies[0, k] = remote(
            x_ref.at[to, head] if split else x_ref,
            place(head, seq),
            send_sem.at[0, k],
            recv_sem.at[0, k],
            {"seq": to},
        )
        copies[0, k].start()
    if split:
        own = pltpu.make_async_copy(x_ref.at[seq], o_ref.at[seq], own_sem)
    else:
        own = pltpu.make_async_copy(x_ref, place(head, seq), own_sem)
    own.start()
    for mask in arrivals(n_head):
        for k in range(1 if split else 0, n_seq):
            if (mask, k) in copies:
                copies[mask, k].wait_recv()
            block = place(masked(head, mask), lax.rem(seq + n_seq - k, n_seq))
            source = x_ref if (mask, k) == (0, 0) else block
            for bit in below(mask, n_head):
                copy = remote(
                    source,
                    block,
                    send_sem.at[mask + bit, k],
                    recv_sem.at[mask + bit, k],
                    {"head": flip(head, bit)},
                )
                copy.start()
                copies[mask + bit, k] = copy
    own.wait()
    if split:
        own = pltpu.make_async_copy(t_ref, to_ref.at[seq], own_sem)
        own.start()
        own.wait()
    for copy in tables:
        copy.wait()
    for copy in copies.values():
        copy.wait_send()


def spread(x, split, ident, table=None):
    n_seq, n_head = lax.axis_size("seq"), lax.axis_size("head")
    rows, cols = x.shape[-2:]
    shape = x.shape if split else (n_head * rows, n_seq * cols)
    shapes = [jax.ShapeDtypeStruct(shape, x.dtype)]
    sem = pltpu.SemaphoreType.DMA
    scratch = [sem((n_head, n_seq)), sem((n_head, n_seq)), sem]
    args = [x]
    if split:
        args.append(table)
        shapes.append(jax.ShapeDtypeStruct((n_seq,) + table.shape, table.dtype))
        scratch.append(sem((2, n_seq)))
    spec = pl.BlockSpec(memory_space=pltpu.VMEM)
    return pl.pallas_call(
        functools.partial(spread_kernel, split),
        out_shape=shapes,
        in_specs=[spec] * len(args),
        out_specs=[spec] * len(args),
        scratch_shapes=scratch,
        compiler_params=pltpu.CompilerParams(collective_id=ident, has_side_effects=True),
    )(*args)


def swap_sum_kernel(x_ref, o_ref, got, total, hand, mixed, send_sem, recv_sem, extra_sems):
    peers, me = lax.axis_size("seq"), lax.axis_index("seq")
    last = peers - 1
    greet([{"seq": lax.rem(me + k, peers)} for k in range(1, peers)])
    relayed = peers >= 4
    ends = (me == 0) | (me == last)
    relay = (me == 1) | (me == last - 1)
    near = jnp.where(me <= 1, 1 - me, 2 * last - 1 - me)
    far = jnp.where(me <= 1, last, 0)
    handed = remote(x_ref.at[far], hand, extra_sems.at[0], extra_sems.at[1], {"seq": near})
    step_far = lax.rem(far - me + peers, peers)
    passed = remote(mixed, got.at[step_far], extra_sems.at[2], recv_sem.at[step_far], {"seq": far})
    if relayed:

        @pl.when(ends)
        def _():
            handed.start()

    copies, direct, coming = [], [], []
    for k in range(1, peers):
        to = lax.rem(me + k, peers)
        copy = remote(x_ref.at[to], got.at[k], send_sem.at[k], recv_sem.at[k], {"seq": to})
        plain = jnp.logical_not((ends | relay) & (to == far)) if relayed else me >= 0
        copies.append(copy)
        direct.append(plain)
        source = lax.rem(me + peers - k, peers)
        coming.append(jnp.logical_not(ends & (source + me == last)) if relayed else me >= 0)
        pl.when(plain)(copy.start)
    if relayed:

        @pl.when(relay)
        def _():
            handed.wait_recv()
            mixed[...] = (
                hand[...].astype(jnp.float32) + x_ref[far].astype(jnp.float32)
            ).astype(mixed.dtype)
            passed.start()

    total[...] = x_ref[me].astype(jnp.float32)
    for k in range(1, peers):

        @pl.when(coming[k - 1])
        def _():
            copies[k - 1].wait_recv()
            total[...] += got[k].astype(jnp.float32)

    o_ref[...] = total[...].astype(o_ref.dtype)
    for copy, plain in zip(copies, direct):
        pl.when(plain)(copy.wait_send)
    if relayed:
        pl.when(ends)(handed.wait_send)
        pl.when(relay)(passed.wait_send)


def swap_sum(x, ident):
    peers, block = x.shape[0], x.shape[1:]
    sem = pltpu.SemaphoreType.DMA
    spec = pl.BlockSpec(memory_space=pltpu.VMEM)
    return pl.pallas_call(
        swap_sum_kernel,
        out_shape=jax.ShapeDtypeStruct(block, x.dtype),
        in_specs=[spec],
        out_specs=spec,
        scratch_shapes=[
            pltpu.VMEM(x.shape, x.dtype),
            pltpu.VMEM(block, jnp.float32),
            pltpu.VMEM(block, x.dtype),
            pltpu.VMEM(block, x.dtype),
            sem((peers,)),
            sem((peers,)),
            sem((3,)),
        ],
        compiler_params=pltpu.CompilerParams(collective_id=ident, has_side_effects=True),
    )(x)


def finish_kernel(
    x_ref, keep_ref, o_ref, held, buf, got, share, pair_sems, seq_sems, head_sems, own_sem
):
    n_seq, n_head = lax.axis_size("seq"), lax.axis_size("head")
    seq, head = lax.axis_index("seq"), lax.axis_index("head")
    top = n_head // 2
    side, peer = head // top, flip(head, top)
    span = share.shape[1]
    bits = [1 << k for k in range(n_head.bit_length() - 1)]
    peers = [{"seq": lax.rem(seq + k, n_seq)} for k in range(1, n_seq)]
    greet(peers + [{"head": flip(head, bit)} for bit in bits])
    order = list(range(1, n_seq)) + [0]
    firsts, swaps = {}, {}
    for k in order:
        to = lax.rem(seq + k, n_seq)
        firsts[k] = remote(
            x_ref.at[1 - side, to], held.at[k], pair_sems.at[0, k], pair_sems.at[1, k],
            {"head": peer},
        )
        firsts[k].start()
    for k in order:
        to = lax.rem(seq + k, n_seq)
        firsts[k].wait_recv()
        value = x_ref[side, to].astype(jnp.float32) + held[k].astype(jnp.float32)
        if k:
            buf[k] = value.astype(buf.dtype)
            swaps[k] = remote(
                buf.at[k], got.at[k], seq_sems.at[0, k], seq_sems.at[1, k], {"seq": to}
            )
            swaps[k].start()
        else:
            total = value + keep_ref[...].astype(jnp.float32)
    for k in range(1, n_seq):
        swaps[k].wait_recv()
        total = total + got[k].astype(jnp.float32)
    share[...] = total.astype(share.dtype)

    def place(head_at):
        return o_ref.at[:, pl.ds(pl.multiple_of(head_at * span, span), span)]

    copies = {}
    for mask in arrivals(n_head):
        if mask in copies:
            copies[mask].wait_recv()
        block = place(masked(head, mask))
        for bit in below(mask, n_head):
            copies[mask + bit] = remote(
                block if mask else share,
                block,
                head_sems.at[0, mask + bit],
                head_sems.at[1, mask + bit],
                {"head": flip(head, bit)},
            )
            copies[mask + bit].start()
    own = pltpu.make_async_copy(share, place(head), own_sem)
    own.start()
    own.wait()
    for copy in (*firsts.values(), *swaps.values(), *copies.values()):
        copy.wait_send()


def finish(sums, keep, ident):
    n_seq, n_head = lax.axis_size("seq"), lax.axis_size("head")
    local, span = keep.shape
    sem = pltpu.SemaphoreType.DMA
    spec = pl.BlockSpec(memory_space=pltpu.VMEM)
    blocks = pltpu.VMEM((n_seq, local, span), sums.dtype)
    return pl.pallas_call(
        finish_kernel,
        out_shape=jax.ShapeDtypeStruct((local, n_head * span), keep.dtype),
        in_specs=[spec] * 2,
        out_specs=spec,
        scratch_shapes=[
            blocks,
            blocks,
            blocks,
            pltpu.VMEM((local, span), keep.dtype),
            sem((2, n_seq)),
            sem((2, n_seq)),
            sem((2, n_head)),
            sem,
        ],
        compiler_params=pltpu.CompilerParams(collective_id=ident, has_side_effects=True),
    )(sums, keep)


def sum_bits(x, axis, bits, ident):
    for k in range(bits):
        x = pair_sum(x.reshape((2, -1) + x.shape[-2:]), axis, 1 << k, ident + k)
    return x


def low_first(index, bits):
    return sum(((index >> k) & 1) << (bits - 1 - k) for k in range(bits))


def moe_kernel(in_ref, pick_ref, mix_ref, gate_ref, up_ref, down_ref, o_ref, x_scr, y_scr):
    expert = pl.program_id(0)
    slots = x_scr.shape[0] // pl.num_programs(0)
    span = o_ref.shape[2]

    @pl.when(expert == 0)
    def _():
        for part in range(o_ref.shape[0]):
            x_scr[:, part * span : (part + 1) * span] = jnp.dot(
                pick_ref[...],
                in_ref[:, part * span : (part + 1) * span],
                preferred_element_type=jnp.float32,
            ).astype(jnp.bfloat16)

    rows = pl.ds(pl.multiple_of(expert * slots, slots), slots)
    x = x_scr[rows, :]
    gate_val = jnp.dot(x, gate_ref[0], preferred_element_type=jnp.float32)
    up_val = jnp.dot(x, up_ref[0], preferred_element_type=jnp.float32)
    hidden = (gate_val * jax.nn.sigmoid(gate_val) * up_val).astype(jnp.bfloat16)
    y_scr[rows, :] = jnp.dot(hidden, down_ref[0], preferred_element_type=jnp.float32).astype(
        jnp.bfloat16
    )

    @pl.when(expert == pl.num_programs(0) - 1)
    def _():
        for part in range(o_ref.shape[0]):
            bits = o_ref.shape[0].bit_length() - 1
            o_ref[low_first(part, bits)] = jnp.dot(
                mix_ref[...],
                y_scr[:, part * span : (part + 1) * span],
                preferred_element_type=jnp.float32,
            ).astype(jnp.bfloat16)


def experts_here(moe_in, pick, mix, expert_gate, expert_up, expert_down, parts):
    amount, wide, inner = expert_gate.shape
    total = moe_in.shape[0]
    fixed = lambda e: (0, 0)
    one = lambda e: (e, 0, 0)
    return pl.pallas_call(
        moe_kernel,
        out_shape=jax.ShapeDtypeStruct((parts, total, wide // parts), jnp.bfloat16),
        grid=(amount,),
        in_specs=[
            pl.BlockSpec(moe_in.shape, fixed),
            pl.BlockSpec(pick.shape, fixed),
            pl.BlockSpec(mix.shape, fixed),
            pl.BlockSpec((1, wide, inner), one),
            pl.BlockSpec((1, wide, inner), one),
            pl.BlockSpec((1, inner, wide), one),
        ],
        out_specs=pl.BlockSpec((parts, total, wide // parts), lambda e: (0, 0, 0)),
        scratch_shapes=[
            pltpu.VMEM((pick.shape[0], wide), jnp.bfloat16),
            pltpu.VMEM((pick.shape[0], wide), jnp.bfloat16),
        ],
        compiler_params=pltpu.CompilerParams(dimension_semantics=("arbitrary",)),
    )(moe_in, pick, mix, expert_gate, expert_up, expert_down)


def slot_tables(route_rows, gate_rows, first, amount, slots):
    total = route_rows.shape[1]
    ids = (first + jnp.arange(amount)).astype(jnp.float32)
    hit = route_rows[None] == ids[:, None, None]
    named = jnp.any(hit, axis=1)
    weight = jnp.sum(jnp.where(hit, gate_rows[None], 0.0), axis=1)
    earlier = (jnp.arange(total)[:, None] < jnp.arange(total)[None, :]).astype(jnp.bfloat16)
    rank = jnp.dot(named.astype(jnp.bfloat16), earlier, preferred_element_type=jnp.float32)
    place = jnp.where(named, rank, -1.0)
    spots = jnp.arange(slots, dtype=jnp.float32)
    pick = (place[:, None, :] == spots[None, :, None]).astype(jnp.bfloat16)
    pick = pick.reshape(amount * slots, total)
    column = jnp.arange(amount * slots)
    spread = (column[None, :] // slots == jnp.arange(amount)[:, None]).astype(jnp.bfloat16)
    wide_place = lax.dot_general(
        place.astype(jnp.bfloat16), spread, (((0,), (0,)), ((), ())),
        preferred_element_type=jnp.float32,
    )
    wide_weight = lax.dot_general(
        weight.astype(jnp.bfloat16), spread, (((0,), (0,)), ((), ())),
        preferred_element_type=jnp.float32,
    )
    spot_of = (column % slots).astype(jnp.float32)
    mix = jnp.where(wide_place == spot_of[None, :], wide_weight, 0.0).astype(jnp.bfloat16)
    return pick, mix


def token_body(
    tokens, attn_weight, attn_gain, moe_gain, routes, gates, expert_gate, expert_up, expert_down
):
    local, width = tokens.shape
    n_seq, n_head = lax.axis_size("seq"), lax.axis_size("head")
    seq, head = lax.axis_index("seq"), lax.axis_index("head")
    total = n_seq * local
    depth, columns = attn_weight.shape[1:]
    own_cols = columns // n_seq
    wide_tokens = tokens.astype(jnp.float32)
    factor = lax.rsqrt(jnp.mean(wide_tokens * wide_tokens, axis=-1) + 1e-06)
    small = jnp.concatenate(
        [routes.T.astype(jnp.float32), gates.T, jnp.broadcast_to(factor[None], (8, local))]
    )
    pieces = tokens.reshape(n_head, local // n_head, n_seq, depth).transpose(2, 0, 1, 3)
    mine, small_all = spread(pieces, True, 2, small)
    mine = mine.reshape(total, depth)
    small_all = small_all.transpose(1, 0, 2).reshape(small.shape[0], total)
    gain = lax.dynamic_slice_in_dim(attn_gain, seq * depth, depth)
    normed = (
        mine.astype(jnp.float32) * small_all[2 * TOPK][:, None] * gain[None]
    ).astype(jnp.bfloat16)
    part = [
        jnp.dot(normed, attn_weight[which], preferred_element_type=jnp.float32)
        .astype(jnp.bfloat16)
        .reshape(total, n_seq, own_cols)
        for which in range(3)
    ]
    part = jnp.stack(part).transpose(2, 0, 1, 3)
    joined = swap_sum(part.reshape(n_seq, 3 * total, own_cols), 3)
    joined = joined.reshape(3, total, own_cols // HEAD_DIM, HEAD_DIM)
    scores = jnp.einsum("thd,shd->hts", joined[0], joined[1], preferred_element_type=jnp.float32)
    lower = jnp.arange(total)[:, None] >= jnp.arange(total)[None, :]
    scores = jnp.where(lower[None], scores, 0.0).astype(jnp.bfloat16)
    outputs = jnp.einsum("hts,she->the", scores, joined[2], preferred_element_type=jnp.float32)
    attended = head_norm(outputs).astype(jnp.bfloat16).reshape(total, own_cols)
    (attended_all,) = swap([attended], [False], "seq", 4)
    attended_all = attended_all.transpose(1, 0, 2).reshape(total, columns)
    out_part = lax.dot_general(
        attended_all, attn_weight[3], (((1,), (1,)), ((), ())), preferred_element_type=jnp.float32
    ).astype(jnp.bfloat16)
    rows = total // n_head
    bits = n_head.bit_length() - 1
    out_part = jnp.stack(
        [out_part[low_first(k, bits) * rows : (low_first(k, bits) + 1) * rows] for k in range(n_head)]
    )
    out_sum = sum_bits(out_part, "head", bits, 5).reshape(rows, depth)
    kept = lax.dynamic_slice_in_dim(mine, head * rows, rows, 0)
    residual_piece = (kept.astype(jnp.float32) + out_sum.astype(jnp.float32)).astype(jnp.bfloat16)
    (residual,) = spread(residual_piece, False, 5 + bits)
    moe_in = rms_scale(residual, moe_gain).astype(jnp.bfloat16)
    amount = expert_gate.shape[0]
    slots = -(-CAP * n_seq // 16) * 16
    pick, mix = slot_tables(
        small_all[:TOPK], small_all[TOPK : 2 * TOPK], seq * amount, amount, slots
    )
    sums = experts_here(moe_in, pick, mix, expert_gate, expert_up, expert_down, n_head)
    span = width // n_head
    pair = sum_bits(sums, "head", bits - 1, 6 + bits).reshape(2, n_seq, local, span)
    own_rows = lax.dynamic_slice(residual, (seq * local, head * span), (local, span))
    return finish(pair, own_rows, 6 + 2 * bits)


def solution(mesh):
    n_seq, n_head = mesh.shape["seq"], mesh.shape["head"]

    def run(tokens, attn_weight, *rest):
        heads_here = attn_weight.shape[2] // HEAD_DIM
        power = n_head & (n_head - 1) == 0 and n_head > 1
        if n_seq > 1 and power and heads_here % n_seq == 0:
            return token_body(tokens, attn_weight, *rest)
        return body(tokens, attn_weight, *rest)

    return jax.shard_map(
        run,
        mesh=mesh,
        in_specs=(
            P(("grp", "seq"), None),
            P(None, "seq", "head"),
            P(),
            P(),
            P(("grp", "seq"), None),
            P(("grp", "seq"), None),
            P("seq", None, "head"),
            P("seq", None, "head"),
            P("seq", "head", None),
        ),
        out_specs=P(("grp", "seq"), None),
        check_vma=False,
    )
```
